256 devices in a mesh: grp: 8 (over y, core), col: 32 (over z, x).
Axes of the slice: x: 4, y: 4, z: 8, core: 2. Of those that a mesh axis runs over, the one named last changes fastest.
Arguments:
- amplitudes: bfloat16 [8, 2048, 1536], P('grp', 'col'), may hold values from -6 to 6
- ladder_int: bfloat16 [8, 1536, 1536], P('grp'), may hold values from -0.15625 to 0.15625
- pair_energy: float32 [8, 1536], P('grp'), may hold values from 0.75 to 1.5
- hole_energy: float32 [8, 2048], P('grp', 'col'), may hold values from 0.75 to 1.5
- pack_map: int32 [6144], P('col'), may hold values from 0 to 191, as said below
- unpack_map: int32 [6144], P('col'), may hold values from 0 to 191, as said below
- coupling_index: int32 [24, 16, 16], P('grp'), may hold values from 0 to 63
- coupling_table: float32 [64], replicated, may hold values from -0.2 to 0.2
- cycle_int: bfloat16 [24, 1024, 1024], P('grp'), may hold values from -0.005859375 to 0.005859375
- tile_list: int32 [8, 8], replicated, may hold values from 0 to 191, as said below
- tile_count: int32 [8], replicated, may hold values from 3 to 8, as said below
- slabs: bfloat16 [8, 8, 128, 1024], P('grp'), may hold values from -0.5 to 0.5
Outputs:
- doubles: bfloat16 [8, 2048, 1536], P('grp', 'col')
- triples: bfloat16 [8, 1024, 1024], P('grp', 'col')
The draws below stay inside these ranges and needn't reach their ends.
Inputs may be any that keep to these rules, and one draw needn't show every extreme that they name: `pack_map`: each column block's 192 entries are a permutation of 0 to 191. `unpack_map`: each column block's 192 entries are a permutation of 0 to 191. `tile_list`: A panel id t lies in channel group t // 24. In each owner's list no channel group is named by more than 2 slots, and in every draw some owner names one group 2 times among its live slots. Slots at or past tile_count are ignored. `tile_count`: in every draw some owner has all 8 slots live and another has 3.
All inputs are finite; a program needn't handle non-finite values.
Results may differ from the reference program's by a relative error of at most 0.04.
Values may be sent and summed in bfloat16 or wider, within the bound.
A program may use at most 128 MiB of HBM per device.

```python
import jax
import jax.numpy as jnp
from jax import lax

P_SIZE = 1536
Q = 2048
R = 1024
MULT = 16
SEG = 512
TILE = 128
SLABW = 1024
NCOEF = 64
ITERS = 4
LMAX = 8
CAPT = 2
CH = 8
PHC = 24
UNITS = 192
N_GRP = 8
N_COL = 32


def block_permutations(key):
    keys = jax.random.split(key, N_COL)
    rows = jax.vmap(lambda single: jax.random.permutation(single, UNITS))(keys)
    return rows.reshape(-1).astype(jnp.int32)


def draw_pack_map(key, part):
    return block_permutations(jax.random.fold_in(key, 11))


def draw_unpack_map(key, part):
    return block_permutations(jax.random.fold_in(key, 13))


def owner_lists(key):
    base = jax.random.fold_in(key, 101)
    keys = jax.random.split(base, 5)
    owners = jnp.arange(N_GRP, dtype=jnp.int32)
    counts = jax.random.randint(keys[0], (N_GRP,), 3, LMAX + 1).astype(jnp.int32)
    fullest = jax.random.randint(keys[1], (), 0, N_GRP).astype(jnp.int32)
    counts = jnp.where(owners == fullest, LMAX, counts)
    counts = jnp.where(owners == (fullest + 1) % N_GRP, 3, counts).astype(jnp.int32)
    group_orders = jax.vmap(lambda single: jax.random.permutation(single, N_GRP))(jax.random.split(keys[2], N_GRP))
    slot_groups = group_orders[:, jnp.arange(LMAX) // CAPT]
    slot_orders = jax.vmap(lambda single: jax.random.permutation(single, LMAX))(jax.random.split(keys[3], N_GRP))
    shuffled = jnp.take_along_axis(slot_groups, slot_orders, axis=1)
    panels_per = 3 * (R // TILE)
    local_ids = jax.random.randint(keys[4], (N_GRP, LMAX), 0, panels_per)
    tiles = (shuffled * panels_per + local_ids).astype(jnp.int32)
    return (counts, tiles)


def draw_tile_list(key, part):
    return owner_lists(key)[1]


def draw_tile_count(key, part):
    return owner_lists(key)[0]


def plant(drawn, key, least, largest):
    longest = drawn.shape.index(max(drawn.shape))
    spots = []
    for shift in (0, 1):
        where = [jax.random.randint(jax.random.fold_in(key, axis), (), 0, length) for axis, length in enumerate(drawn.shape)]
        where[longest] = (where[longest] + shift) % drawn.shape[longest]
        spots.append(tuple(where))
    return drawn.at[spots[0]].set(least).at[spots[1]].set(largest)


def level_of(stream_key, shape, shards, low, top_value):
    factor_of, own = 1.0, jax.random.fold_in(stream_key, 6)
    for dim, shards_of in shards:
        draws = jnp.exp(jax.random.uniform(jax.random.fold_in(own, dim), (shards_of,), jnp.float32, low / len(shards), top_value / len(shards)))
        factor_of = factor_of * jnp.repeat(draws, shape[dim] // shards_of).reshape([-1 if axis == dim else 1 for axis in range(len(shape))])
    return factor_of


def centred(stream_key, shape, scale, most, cuts=(), held_as=jnp.bfloat16):
    array = jax.random.normal(stream_key, shape, jnp.float32) * scale
    if len(cuts) > 0:
        array = level_of(stream_key, shape, cuts, -0.22, 0.18) * array
    return jnp.clip(array, min=-most, max=most).astype(held_as)


def setup_inputs(seed: int = 0) -> dict:
    key_of = jax.random.split(jax.random.key(seed), 13)
    amplitudes = centred(key_of[0], (CH, Q, P_SIZE), 1.0, 6.0, ((0, 8), (1, 32)))
    ladder_int = centred(key_of[1], (CH, P_SIZE, P_SIZE), P_SIZE ** -0.5, 0.15625, ((0, 8),))
    pair_energy = jnp.clip(0.75 + 0.75 * jax.random.uniform(key_of[2], (CH, P_SIZE), jnp.float32) ** level_of(key_of[2], (CH, P_SIZE), ((0, 8),), -0.2, 0.2), 0.75, 1.5)
    hole_energy = jnp.clip(0.75 + 0.75 * jax.random.uniform(key_of[3], (CH, Q), jnp.float32) ** level_of(key_of[3], (CH, Q), ((0, 8), (1, 32)), -0.2, 0.2), 0.75, 1.5)
    pack_map = draw_pack_map(jax.random.fold_in(key_of[12], 71), 0)
    unpack_map = draw_unpack_map(jax.random.fold_in(key_of[12], 71), 0)
    coupling_index = plant(jax.random.randint(key_of[6], (PHC, MULT, MULT), 0, NCOEF), jax.random.fold_in(key_of[6], 1), 0, NCOEF - 1).astype(jnp.int32)
    coupling_table = jnp.clip(jax.random.uniform(key_of[7], (NCOEF,), jnp.float32, -0.2, 0.2), -0.2, 0.2)
    cycle_int = centred(key_of[8], (PHC, R, R), (R * R) ** -0.5, 0.005859375, ((0, 8),))
    tile_list = draw_tile_list(jax.random.fold_in(key_of[12], 71), 0)
    tile_count = draw_tile_count(jax.random.fold_in(key_of[12], 71), 0)
    slabs = centred(key_of[11], (N_GRP, LMAX, TILE, SLABW), TILE ** -0.5, 0.5, ((0, 8),))
    return {"amplitudes": amplitudes, "ladder_int": ladder_int, "pair_energy": pair_energy, "hole_energy": hole_energy, "pack_map": pack_map, "unpack_map": unpack_map, "coupling_index": coupling_index, "coupling_table": coupling_table, "cycle_int": cycle_int, "tile_list": tile_list, "tile_count": tile_count, "slabs": slabs}


def pick_rows(table, order):
    return table[order]


def place_rows(table, order):
    return jnp.zeros_like(table).at[order].set(table)


def reference(amplitudes, ladder_int, pair_energy, hole_energy, pack_map, unpack_map, coupling_index, coupling_table, cycle_int, tile_list, tile_count, slabs):
    col_count = N_COL
    per_peer = UNITS // col_count
    packs = pack_map.reshape(col_count, UNITS)
    unpacks = unpack_map.reshape(col_count, UNITS)
    pick_all = jax.vmap(pick_rows)
    place_all = jax.vmap(place_rows)

    def swap_blocks(blocks):
        return blocks.reshape(col_count, col_count, per_peer, SEG).transpose(1, 0, 2, 3).reshape(col_count, UNITS, SEG)

    def forward(matrix):
        segments = matrix.reshape(col_count, UNITS, SEG)
        arrived = swap_blocks(pick_all(segments, packs))
        columns = pick_all(arrived, unpacks).reshape(R, 3, R)
        return columns.transpose(1, 0, 2)

    def backward(columns):
        segments = columns.transpose(1, 0, 2).reshape(col_count, UNITS, SEG)
        arrived = swap_blocks(place_all(segments, unpacks))
        return place_all(arrived, packs).reshape(Q, P_SIZE)

    coeffs = coupling_table[coupling_index]
    denom = pair_energy[:, None, :] + hole_energy[:, :, None]
    source = amplitudes.astype(jnp.float32)
    channels = 3 * N_GRP

    def ladder_one(pair):
        return jnp.dot(pair[0], pair[1], preferred_element_type=jnp.float32)

    def cycle_one(pair):
        half = jnp.dot(pair[0], pair[1], preferred_element_type=jnp.float32).astype(jnp.bfloat16)
        return jnp.dot(half, pair[0], preferred_element_type=jnp.float32).astype(jnp.bfloat16)

    doubles = amplitudes
    cycle = jnp.zeros((channels, R, R), jnp.bfloat16)
    for iteration in range(ITERS):
        ladder = lax.map(ladder_one, (doubles, ladder_int))
        regrouped = jax.vmap(forward)(doubles).reshape(channels, R, R)
        spread = regrouped.astype(jnp.float32).reshape(channels, R, R // MULT, MULT)
        mixed = jnp.einsum('euan,emn->euam', spread, coeffs, precision=lax.Precision.HIGHEST)
        recoupled = (spread + mixed).reshape(channels, R, R).astype(jnp.bfloat16)
        cycle = lax.map(cycle_one, (recoupled, cycle_int))
        returned = jax.vmap(backward)(cycle.reshape(N_GRP, 3, R, R))
        doubles = ((source + ladder + returned.astype(jnp.float32)) / denom).astype(jnp.bfloat16)
    blocks_per = R // TILE
    panels = cycle.reshape(channels, R, blocks_per, TILE).transpose(0, 2, 1, 3).reshape(channels * blocks_per, R, TILE)
    live = (jnp.arange(LMAX, dtype=jnp.int32)[None, :] < tile_count[:, None]).astype(jnp.float32)
    chosen = panels[tile_list].astype(jnp.float32) * live[:, :, None, None]
    triples = jnp.einsum('hsui,hsin->hun', chosen, slabs.astype(jnp.float32)).astype(jnp.bfloat16)
    return doubles, triples
```

```python
import functools

import jax
import jax.numpy as jnp
from jax import lax
from jax.experimental import pallas as pl
from jax.experimental.pallas import tpu as pltpu
from jax.sharding import PartitionSpec as P

MULT = 16
SEG = 512
TILE = 128
ITERS = 4
NX = 4
NZ = 8
PER = 6
ZROWS = NX * PER
UNITS = 192
PLANE = NX * UNITS
ROWS = 32
CHUNK = NX * ROWS
PH = 3
MESH = pl.DeviceIdType.MESH
F32 = jnp.float32
BF16 = jnp.bfloat16


def dot(a, b):
    return jnp.dot(a, b, preferred_element_type=F32)


def kernel(
    n_grp,
    amp,
    pair_e,
    hole_e,
    pack_row,
    pack_col,
    slots_own,
    coef_index,
    table,
    tile_list,
    tile_count,
    w_hbm,
    l_hbm,
    slab_hbm,
    d_out,
    t_out,
    w,
    lint,
    slab,
    kron,
    slots,
    perm,
    perm_t,
    pack,
    pack_t,
    doubles,
    ladder,
    packed,
    segs,
    cols,
    panel,
    xrow,
    half,
    cyc,
    slotted,
    back_z,
    back_x,
    own_rows,
    pick,
    picked,
    local_sem,
    slots_sem,
    fz_sem,
    fk_sem,
    fx_sem,
    ring_sem,
    bz_sem,
    bx_sem,
    tx_sem,
    tg_sem,
):
    me = lax.axis_index("col")
    g = lax.axis_index("grp")
    z = me // NX
    x = me % NX

    def at_z(d):
        return (z + d + NZ) % NZ

    def at_x(d):
        return (x + d + NX) % NX

    def remote(src, dst, sems, index, grp, zz, xx):
        return pltpu.make_async_remote_copy(
            src_ref=src,
            dst_ref=dst,
            send_sem=sems.at[(0,) + index],
            recv_sem=sems.at[(1,) + index],
            device_id=(grp, zz * NX + xx),
            device_id_type=MESH,
        )

    loads = [
        pltpu.make_async_copy(l_hbm, lint, local_sem.at[0]),
        pltpu.make_async_copy(w_hbm, w, local_sem.at[1]),
        pltpu.make_async_copy(slab_hbm, slab, local_sem.at[2]),
    ]
    for load in loads:
        load.start()

    barrier = pltpu.get_barrier_semaphore()
    for d in range(1, NZ):
        pl.semaphore_signal(
            barrier, inc=1, device_id=(g, at_z(d) * NX + x), device_id_type=MESH
        )
    for d in range(1, NX):
        pl.semaphore_signal(
            barrier, inc=1, device_id=(g, z * NX + at_x(d)), device_id_type=MESH
        )
    for d in range(1, n_grp):
        pl.semaphore_signal(
            barrier, inc=1, device_id=((g + d) % n_grp, me), device_id_type=MESH
        )

    lane_k = lax.broadcasted_iota(jnp.int32, (UNITS, UNITS), 1)
    row_k = lax.broadcasted_iota(jnp.int32, (UNITS, UNITS), 0)
    lane_k = (lane_k % 64) * 3 + lane_k // 64
    row_k = (row_k % 64) * 3 + row_k // 64
    pack[...] = (pack_col[...] == lane_k).astype(F32).astype(BF16)
    pack_t[...] = (pack_row[...] == row_k).astype(F32).astype(BF16)
    for t in range(3):
        doubles[t * 64 : (t + 1) * 64, :] = amp[:, t * SEG : (t + 1) * SEG]

    pl.semaphore_wait(barrier, (NZ - 1) + (NX - 1) + (n_grp - 1))

    def slots_copy(d, to):
        return remote(
            slots_own, slots.at[x if to else at_x(-d)], slots_sem, (d,), g, z, at_x(d)
        )

    for d in range(1, NX):
        slots_copy(d, True).start()
    slots[x] = slots_own[...]

    def forward_z(d, to):
        target = at_z(d)
        return remote(
            packed.at[target], segs.at[z if to else at_z(-d), x], fz_sem, (d,), g, target, x
        )

    def send_packed():
        value = dot(pack[...], doubles[...])
        for zz in range(NZ):
            packed[zz] = value[zz * ZROWS : (zz + 1) * ZROWS, :].astype(BF16)
        for d in (4, 3, 5, 2, 6, 1, 7):
            forward_z(d, True).start()
        segs[z, x] = packed[z]

    def ladder_part():
        for t in range(3):
            acc = None
            for k in range(3):
                part = dot(
                    doubles[k * 64 : (k + 1) * 64, :],
                    lint[k * SEG : (k + 1) * SEG, t * SEG : (t + 1) * SEG],
                )
                acc = part if acc is None else acc + part
            ladder[:, t * SEG : (t + 1) * SEG] = acc

    def forward_k(d, to):
        target = at_x(d)
        lanes = pl.ds(pl.multiple_of(target * TILE, TILE), TILE)
        return remote(
            segs.at[:, x, :, lanes],
            cols.at[:, x if to else at_x(-d)],
            fk_sem,
            (d,),
            g,
            z,
            target,
        )

    def forward_x(d, to):
        source = x if to else at_x(-d)
        return remote(
            segs.at[:, x], segs.at[:, source], fx_sem, (d,), g, z, at_x(d)
        )

    def ring(way, step, e, to):
        sign = 1 if way == 0 else -1
        chunk = at_z(-sign * (step - 1)) if to else at_z(-sign * step)
        if step < 4:
            rows = pl.ds(pl.multiple_of(chunk * CHUNK, CHUNK), CHUNK)
        else:
            rows = pl.ds(pl.multiple_of(chunk * CHUNK + way * 64, 64), 64)
        ref = panel.at[e, rows, :]
        return remote(ref, ref, ring_sem, (way, step - 1, e), g, at_z(sign), x)

    def recouple(value, e):
        mixed = dot(value.astype(BF16), kron[e])
        return (value + (mixed[:, :TILE] + mixed[:, TILE:])).astype(BF16)

    def row_part(e):
        found = dot(
            perm[e * 256 : (e + 1) * 256, :],
            segs[...].reshape(PLANE, SEG),
        )
        stacked = jnp.concatenate(
            [found[:, q * TILE : (q + 1) * TILE] for q in range(4)], axis=0
        )
        done = recouple(stacked, e)
        for q in range(4):
            for h in range(2):
                xrow[e, :, (h * 4 + q) * TILE : (h * 4 + q + 1) * TILE] = done[
                    q * 256 + h * CHUNK : q * 256 + (h + 1) * CHUNK, :
                ]

    def half_part(e):
        half[e] = dot(xrow[e], w[e]).astype(BF16)

    def backward_z(d, to):
        target = at_z(d)
        return remote(
            slotted.at[target],
            back_z.at[z if to else at_z(-d)],
            bz_sem,
            (d,),
            g,
            target,
            x,
        )

    def backward_x(d, to):
        target = at_x(d)
        return remote(
            back_z.at[:, target],
            back_x.at[x if to else at_x(-d)],
            bx_sem,
            (d,),
            g,
            z,
            target,
        )

    def own_copy(d, to):
        target = at_x(d)
        return remote(
            cyc.at[:, target],
            own_rows.at[x if to else at_x(-d)],
            tx_sem,
            (d,),
            g,
            z,
            target,
        )

    def group_copy(d, to):
        target = (g + d) % n_grp
        source = g if to else (g - d + n_grp) % n_grp
        return remote(pick.at[d], picked.at[source], tg_sem, (d,), target, z, x)

    send_packed()

    def coef_step(k, acc):
        return jnp.where(coef_index[...] == k, table[k], acc)

    coefs = lax.fori_loop(
        0, table.shape[0], coef_step, jnp.zeros((PH, TILE, TILE), F32)
    )
    same = (
        lax.broadcasted_iota(jnp.int32, (PH, TILE, TILE), 1) // MULT
        == lax.broadcasted_iota(jnp.int32, (PH, TILE, TILE), 2) // MULT
    )
    coefs = jnp.where(same, coefs, 0.0)
    high = coefs.astype(BF16)
    kron[:, :, :TILE] = high
    kron[:, :, TILE:] = (coefs - high.astype(F32)).astype(BF16)

    for d in range(1, NX):
        slots_copy(d, False).wait_recv()
    lane_x = lax.broadcasted_iota(jnp.int32, (8, TILE), 1) // ROWS
    place = jnp.zeros((8, TILE), F32)
    for xx in range(NX):
        place = jnp.where(lane_x == xx, slots[xx] + float(PER * xx), place)
    for k in range(2 * PH):
        line = place[k : k + 1, :]
        index = lax.broadcasted_iota(jnp.int32, (PLANE, TILE), 0).astype(F32)
        perm_t[:, k * TILE : (k + 1) * TILE] = (index == line).astype(F32).astype(BF16)
        column = jnp.transpose(jnp.broadcast_to(line, (TILE, TILE)))
        for b in range(PLANE // TILE):
            lanes = lax.broadcasted_iota(jnp.int32, (TILE, TILE), 1) + b * TILE
            perm[k * TILE : (k + 1) * TILE, b * TILE : (b + 1) * TILE] = (
                (column == lanes.astype(F32)).astype(F32).astype(BF16)
            )

    loads[0].wait()

    def iteration(it, carry):
        @pl.when(it > 0)
        def _():
            send_packed()

        ladder_part()
        for d in (1, 7, 2, 6, 3, 5, 4):
            forward_z(d, False).wait_recv()
        for d in (2, 1, 3):
            forward_k(d, True).start()
        for d in (2, 1, 3):
            forward_x(d, True).start()
        cols[:, x] = segs[:, x, :, pl.ds(pl.multiple_of(x * TILE, TILE), TILE)]
        for d in (1, 3, 2):
            forward_k(d, False).wait_recv()
        found = dot(perm[...], cols[...].reshape(PLANE, TILE))
        for e in range(PH):
            done = recouple(found[e * 256 : (e + 1) * 256, :], e)
            rows = pl.ds(pl.multiple_of(z * CHUNK, CHUNK), CHUNK)
            panel[e, rows, :TILE] = done[:CHUNK, :]
            panel[e, rows, TILE:] = done[CHUNK:, :]
            ring(0, 1, e, True).start()
            ring(1, 1, e, True).start()
        for e in range(PH):
            for way in range(2):
                ring(way, 1, e, False).wait_recv()
                ring(way, 2, e, True).start()
        for d in (1, 3, 2):
            forward_x(d, False).wait_recv()

        @pl.when(it == 0)
        def _():
            loads[1].wait()

        for e in range(PH):
            for way in range(2):
                ring(way, 2, e, False).wait_recv()
                ring(way, 3, e, True).start()
            row_part(e)
        for e in range(PH):
            for way in range(2):
                ring(way, 3, e, False).wait_recv()
                ring(way, 4, e, True).start()
            half_part(e)
        for e in range(PH):
            for way in range(2):
                ring(way, 4, e, False).wait_recv()
            block = dot(half[e], panel[e])
            for h in range(2):
                cyc[2 * e + h] = (
                    block[:, h * TILE : (h + 1) * TILE]
                    .reshape(NX, ROWS, TILE)
                    .astype(BF16)
                )
        value = dot(perm_t[...], cyc[...].reshape(PLANE, TILE))
        slotted[...] = value.reshape(NZ, NX, ZROWS, TILE).astype(BF16)
        for d in range(1, NX):
            forward_k(d, True).wait_send()
            forward_x(d, True).wait_send()
        for d in (4, 3, 5, 2, 6, 1, 7):
            backward_z(d, True).start()
        back_z[z] = slotted[z]

        @pl.when(it == ITERS - 1)
        def _():
            for d in (2, 1, 3):
                own_copy(d, True).start()
            own_rows[x] = cyc[:, x]

        for d in (1, 7, 2, 6, 3, 5, 4):
            backward_z(d, False).wait_recv()
        for d in (2, 1, 3):
            backward_x(d, True).start()
        back_x[x] = back_z[:, x]

        @pl.when(it == ITERS - 1)
        def _():
            for d in (1, 3, 2):
                own_copy(d, False).wait_recv()
            for d in range(n_grp):
                owner = (g + d) % n_grp
                count = jnp.int32(0)
                first = jnp.int32(0)
                second = jnp.int32(0)
                for s in range(tile_list.shape[1]):
                    tile = tile_list[owner, s]
                    mine = tile // 24 == g
                    local = tile - g * 24
                    blk = local % 8
                    where = (blk % 4) * (2 * PH) + (local // 8) * 2 + blk // 4
                    first = jnp.where(mine & (count == 0), where, first)
                    second = jnp.where(mine & (count == 1), where, second)
                    count = count + jnp.where(mine, 1, 0)
                flat = own_rows.reshape(NX * 2 * PH, ROWS, TILE)
                if d == 0:
                    picked[g, 0] = flat[first]
                    picked[g, 1] = flat[second]
                else:
                    pick[d, 0] = flat[first]
                    pick[d, 1] = flat[second]
                    group_copy(d, True).start()

        for d in (1, 3, 2):
            backward_x(d, False).wait_recv()
        together = jnp.concatenate(
            [back_x[xx].reshape(UNITS, TILE) for xx in range(NX)], axis=1
        )
        returned = dot(pack_t[...], together)
        for t in range(3):
            lanes = slice(t * SEG, (t + 1) * SEG)
            total = (amp[:, lanes].astype(F32) + ladder[:, lanes]) + returned[
                t * 64 : (t + 1) * 64, :
            ]
            doubles[t * 64 : (t + 1) * 64, :] = (
                total / (pair_e[:, lanes] + hole_e[...])
            ).astype(BF16)

        for d in range(1, NZ):
            forward_z(d, True).wait_send()
            backward_z(d, True).wait_send()
        for d in range(1, NX):
            backward_x(d, True).wait_send()
        for step in range(1, 5):
            for e in range(PH):
                for way in range(2):
                    ring(way, step, e, True).wait_send()
        return carry

    lax.fori_loop(0, ITERS, iteration, jnp.int32(0))

    for t in range(3):
        d_out[:, t * SEG : (t + 1) * SEG] = doubles[t * 64 : (t + 1) * 64, :]

    for d in range(1, n_grp):
        group_copy(d, False).wait_recv()
    loads[2].wait()
    live = tile_count[g]
    flat = picked.reshape(n_grp * 2, ROWS, TILE)
    parts = []
    for s in range(tile_list.shape[1]):
        group = tile_list[g, s] // 24
        rank = jnp.int32(0)
        for before in range(s):
            rank = rank + jnp.where(tile_list[g, before] // 24 == group, 1, 0)
        part = flat[group * 2 + jnp.minimum(rank, 1)]
        parts.append(
            (part.astype(F32) * jnp.where(s < live, 1.0, 0.0).astype(F32)).astype(BF16)
        )
    t_out[...] = dot(jnp.concatenate(parts, axis=1), slab[...]).astype(BF16)

    for d in range(1, NX):
        slots_copy(d, True).wait_send()
        own_copy(d, True).wait_send()
    for d in range(1, n_grp):
        group_copy(d, True).wait_send()


def body(
    amplitudes,
    ladder_int,
    pair_energy,
    hole_energy,
    pack_map,
    unpack_map,
    coupling_index,
    coupling_table,
    cycle_int,
    tile_list,
    tile_count,
    slabs,
):
    n_grp = lax.axis_size("grp")
    width_p = amplitudes.shape[2]
    width_r = cycle_int.shape[1]
    slot = (unpack_map // PER) * ZROWS + unpack_map % PER
    slot = slot.reshape(ROWS, 2 * PH).transpose(1, 0).astype(F32)
    slots_own = jnp.pad(jnp.tile(slot, (1, NX)), ((0, 2), (0, 0)))
    coef_index = jnp.tile(jnp.swapaxes(coupling_index, 1, 2), (1, 8, 8))

    vmem = pl.BlockSpec(memory_space=pltpu.VMEM)
    smem = pl.BlockSpec(memory_space=pltpu.SMEM)
    anywhere = pl.BlockSpec(memory_space=pl.ANY)
    dma = pltpu.SemaphoreType.DMA
    doubles, triples = pl.pallas_call(
        functools.partial(kernel, n_grp),
        out_shape=(
            jax.ShapeDtypeStruct((64, width_p), BF16),
            jax.ShapeDtypeStruct((ROWS, width_r), BF16),
        ),
        in_specs=[vmem] * 7 + [smem] * 3 + [anywhere] * 3,
        out_specs=(vmem, vmem),
        scratch_shapes=[
            pltpu.VMEM((PH, width_r, width_r), BF16),
            pltpu.VMEM((width_p, width_p), BF16),
            pltpu.VMEM((width_r, width_r), BF16),
            pltpu.VMEM((PH, TILE, 2 * TILE), BF16),
            pltpu.VMEM((NX, 8, TILE), F32),
            pltpu.VMEM((PLANE, PLANE), BF16),
            pltpu.VMEM((PLANE, PLANE), BF16),
            pltpu.VMEM((UNITS, UNITS), BF16),
            pltpu.VMEM((UNITS, UNITS), BF16),
            pltpu.VMEM((UNITS, SEG), BF16),
            pltpu.VMEM((64, width_p), F32),
            pltpu.VMEM((NZ, ZROWS, SEG), BF16),
            pltpu.VMEM((NZ, NX, ZROWS, SEG), BF16),
            pltpu.VMEM((NZ, NX, ZROWS, TILE), BF16),
            pltpu.VMEM((PH, width_r, 2 * TILE), BF16),
            pltpu.VMEM((PH, CHUNK, width_r), BF16),
            pltpu.VMEM((PH, CHUNK, width_r), BF16),
            pltpu.VMEM((2 * PH, NX, ROWS, TILE), BF16),
            pltpu.VMEM((NZ, NX, ZROWS, TILE), BF16),
            pltpu.VMEM((NZ, NX, ZROWS, TILE), BF16),
            pltpu.VMEM((NX, NZ, ZROWS, TILE), BF16),
            pltpu.VMEM((NX, 2 * PH, ROWS, TILE), BF16),
            pltpu.VMEM((n_grp, 2, ROWS, TILE), BF16),
            pltpu.VMEM((n_grp, 2, ROWS, TILE), BF16),
            dma((3,)),
            dma((2, NX)),
            dma((2, NZ)),
            dma((2, NX)),
            dma((2, NX)),
            dma((2, 2, 4, PH)),
            dma((2, NZ)),
            dma((2, NX)),
            dma((2, NX)),
            dma((2, n_grp)),
        ],
        compiler_params=pltpu.CompilerParams(
            collective_id=0, has_side_effects=True, vmem_limit_bytes=60 * 1024 * 1024
        ),
    )(
        amplitudes[0],
        pair_energy,
        hole_energy.reshape(-1, 1),
        pack_map.reshape(1, -1),
        pack_map.reshape(-1, 1),
        slots_own,
        coef_index,
        coupling_table,
        tile_list,
        tile_count,
        cycle_int,
        ladder_int[0],
        slabs.reshape(width_r, width_r),
    )
    return doubles[None], triples[None]


def solution(mesh):
    return jax.shard_map(
        body,
        mesh=mesh,
        in_specs=(
            P("grp", "col", None),
            P("grp", None, None),
            P("grp", None),
            P("grp", "col"),
            P("col"),
            P("col"),
            P("grp", None, None),
            P(),
            P("grp", None, None),
            P(),
            P(),
            P("grp", None, None, None),
        ),
        out_specs=(P("grp", "col", None), P("grp", "col", None)),
        check_vma=False,
    )
```

```python
import functools

import jax
import jax.numpy as jnp
from jax import lax
from jax.experimental import pallas as pl
from jax.experimental.pallas import tpu as pltpu
from jax.sharding import PartitionSpec as P

MULT = 16
SEG = 512
TILE = 128
ITERS = 4
NX = 4
NZ = 8
PER = 6
ZROWS = NX * PER
UNITS = 192
PLANE = NX * UNITS
ROWS = 32
CHUNK = NX * ROWS
PH = 3
MESH = pl.DeviceIdType.MESH
F32 = jnp.float32
BF16 = jnp.bfloat16


def dot(a, b):
    return jnp.dot(a, b, preferred_element_type=F32)


def kernel(
    n_grp,
    amp,
    pair_e,
    hole_e,
    pack_row,
    unpack_row,
    coef_index,
    table,
    tile_list,
    tile_count,
    w_hbm,
    l_hbm,
    slab_hbm,
    d_out,
    t_out,
    w,
    lint,
    slab,
    kron,
    slots,
    hole,
    perm,
    perm_t,
    pack,
    pack_t,
    doubles,
    ladder,
    packed,
    cols,
    panel,
    rows_in,
    half,
    cyc,
    slotted,
    back,
    own_rows,
    pick,
    picked,
    local_sem,
    slots_sem,
    forward_sem,
    row_sem,
    ring_sem,
    backward_sem,
    tx_sem,
    tg_sem,
):
    me = lax.axis_index("col")
    g = lax.axis_index("grp")
    z = me // NX
    x = me % NX

    def at_z(d):
        return (z + d + NZ) % NZ

    def at_x(d):
        return (x + d + NX) % NX

    def remote(src, dst, sems, index, grp, zz, xx):
        return pltpu.make_async_remote_copy(
            src_ref=src,
            dst_ref=dst,
            send_sem=sems.at[(0,) + index],
            recv_sem=sems.at[(1,) + index],
            device_id=(grp, zz * NX + xx),
            device_id_type=MESH,
        )

    others = [(dz, dx) for dz in (4, 3, 5, 2, 6, 1, 7, 0) for dx in (2, 1, 3, 0)][:-1]

    loads = [
        pltpu.make_async_copy(l_hbm, lint, local_sem.at[0]),
        pltpu.make_async_copy(w_hbm, w, local_sem.at[1]),
        pltpu.make_async_copy(slab_hbm, slab, local_sem.at[2]),
    ]
    for load in loads:
        load.start()

    barrier = pltpu.get_barrier_semaphore()
    for dz, dx in others:
        pl.semaphore_signal(
            barrier, inc=1, device_id=(g, at_z(dz) * NX + at_x(dx)), device_id_type=MESH
        )
    for d in range(1, n_grp):
        pl.semaphore_signal(
            barrier, inc=1, device_id=((g + d) % n_grp, me), device_id_type=MESH
        )

    def iota(shape, axis):
        return lax.broadcasted_iota(jnp.int32, shape, axis)

    def one_hot(match):
        return match.astype(F32).astype(BF16)

    def as_column(row):
        size = row.shape[1]
        eye = iota((size, size), 0) == iota((size, size), 1)
        return jnp.sum(jnp.where(eye, row, 0.0), axis=1, keepdims=True)

    pack_line = pack_row[...].astype(F32)
    lane_k = iota((UNITS, UNITS), 1)
    row_k = iota((UNITS, UNITS), 0)
    lane_k = (lane_k % 64) * 3 + lane_k // 64
    row_k = (row_k % 64) * 3 + row_k // 64
    pack[...] = one_hot(as_column(pack_line) == lane_k.astype(F32))
    for t in range(3):
        doubles[t * 64 : (t + 1) * 64, :] = amp[:, t * SEG : (t + 1) * SEG]

    pl.semaphore_wait(barrier, len(others) + (n_grp - 1))

    def slots_copy(d, to):
        return remote(
            unpack_row, slots.at[x if to else at_x(-d)], slots_sem, (d,), g, z, at_x(d)
        )

    def forward(dz, dx, to):
        zz, xx = at_z(dz), at_x(dx)
        place = cols.at[z, x] if to else cols.at[at_z(-dz), at_x(-dx)]
        return remote(packed.at[zz, xx], place, forward_sem, (dz, dx), g, zz, xx)

    def send_packed():
        value = dot(pack[...], doubles[...])
        for zz in range(NZ):
            for xx in range(NX):
                packed[zz, xx] = value[
                    zz * ZROWS : (zz + 1) * ZROWS, xx * TILE : (xx + 1) * TILE
                ].astype(BF16)
        for dz, dx in others:
            forward(dz, dx, True).start()
        cols[z, x] = packed[z, x]

    def ladder_part():
        for t in range(3):
            acc = None
            for k in range(3):
                part = dot(
                    doubles[k * 64 : (k + 1) * 64, :],
                    lint[k * SEG : (k + 1) * SEG, t * SEG : (t + 1) * SEG],
                )
                acc = part if acc is None else acc + part
            ladder[:, t * SEG : (t + 1) * SEG] = acc

    def row_copy(d, e, to):
        rows = pl.ds(pl.multiple_of(z * CHUNK, CHUNK), CHUNK)
        return remote(
            panel.at[e, rows, :],
            rows_in.at[x if to else at_x(-d), e],
            row_sem,
            (d, e),
            g,
            z,
            at_x(d),
        )

    def ring(way, step, e, to):
        sign = 1 if way == 0 else -1
        chunk = at_z(-sign * (step - 1)) if to else at_z(-sign * step)
        if step < 4:
            rows = pl.ds(pl.multiple_of(chunk * CHUNK, CHUNK), CHUNK)
        else:
            rows = pl.ds(pl.multiple_of(chunk * CHUNK + way * 64, 64), 64)
        ref = panel.at[e, rows, :]
        return remote(ref, ref, ring_sem, (way, step - 1, e), g, at_z(sign), x)

    def recouple(value, e):
        mixed = dot(value.astype(BF16), kron[e])
        return (value + (mixed[:, :TILE] + mixed[:, TILE:])).astype(BF16)

    def half_part(e):
        value = jnp.concatenate(
            [
                rows_in[xx, e, :, h * TILE : (h + 1) * TILE]
                for h in range(2)
                for xx in range(NX)
            ],
            axis=1,
        )
        half[e] = dot(value, w[e]).astype(BF16)

    def backward(dz, dx, to):
        zz, xx = at_z(dz), at_x(dx)
        place = back.at[z, x] if to else back.at[at_z(-dz), at_x(-dx)]
        return remote(slotted.at[zz, xx], place, backward_sem, (dz, dx), g, zz, xx)

    def own_copy(d, to):
        target = at_x(d)
        return remote(
            cyc.at[:, target],
            own_rows.at[x if to else at_x(-d)],
            tx_sem,
            (d,),
            g,
            z,
            target,
        )

    def group_copy(d, to):
        target = (g + d) % n_grp
        source = g if to else (g - d + n_grp) % n_grp
        return remote(pick.at[d], picked.at[source], tg_sem, (d,), target, z, x)

    for d in range(1, NX):
        slots_copy(d, True).start()
    send_packed()
    slots[x] = unpack_row[...]

    pack_t[...] = one_hot(pack_line == row_k.astype(F32))
    hole[...] = jnp.broadcast_to(as_column(hole_e[...]), hole.shape)

    def coef_step(k, acc):
        return jnp.where(coef_index[...] == k, table[k], acc)

    coefs = lax.fori_loop(
        0, table.shape[0], coef_step, jnp.zeros((PH, MULT, MULT), F32)
    )
    spread = one_hot(iota((TILE, MULT), 0) % MULT == iota((TILE, MULT), 1))
    same = iota((TILE, TILE), 0) // MULT == iota((TILE, TILE), 1) // MULT
    turned = (((1,), (1,)), ((), ()))
    for e in range(PH):
        high = coefs[e].astype(BF16)
        low = (coefs[e] - high.astype(F32)).astype(BF16)
        for i, part in enumerate((high, low)):
            tall = lax.dot_general(spread, part, turned, preferred_element_type=F32)
            full = lax.dot_general(
                tall.astype(BF16), spread, turned, preferred_element_type=F32
            )
            kron[e, :, i * TILE : (i + 1) * TILE] = jnp.where(same, full, 0.0).astype(
                BF16
            )

    for d in range(1, NX):
        slots_copy(d, False).wait_recv()
    raw = jnp.concatenate(
        [slots[xx] for xx in range(NX)] + [slots[xx] for xx in range(NX)], axis=0
    )
    raw = raw.astype(F32).astype(BF16)
    mine = iota((8, TILE), 0) == iota((8, TILE), 1) // ROWS
    owner = iota((1, TILE), 1) // ROWS
    for k in range(2 * PH):
        select = one_hot(
            iota((UNITS, TILE), 0) == (iota((UNITS, TILE), 1) % ROWS) * 2 * PH + k
        )
        found = jnp.where(mine, dot(raw, select), 0.0)
        unit = jnp.sum(found, axis=0, keepdims=True).astype(jnp.int32)
        line = (unit // PER) * ZROWS + unit % PER + owner * PER
        perm_t[:, k * TILE : (k + 1) * TILE] = one_hot(iota((PLANE, TILE), 0) == line)
        column = as_column(line.astype(F32)).astype(jnp.int32)
        perm[k * TILE : (k + 1) * TILE, :] = one_hot(iota((TILE, PLANE), 1) == column)

    loads[0].wait()

    def iteration(it, carry):
        @pl.when(it > 0)
        def _():
            send_packed()

        ladder_part()
        for dz, dx in reversed(others):
            forward(dz, dx, False).wait_recv()
        arrived = cols[...].reshape(PLANE, TILE)
        for e in range(PH):
            found = dot(perm[e * 256 : (e + 1) * 256, :], arrived)
            done = recouple(found, e)
            rows = pl.ds(pl.multiple_of(z * CHUNK, CHUNK), CHUNK)
            for h in range(2):
                lanes = slice(h * TILE, (h + 1) * TILE)
                panel[e, rows, lanes] = done[h * CHUNK : (h + 1) * CHUNK, :]
                rows_in[x, e, :, lanes] = done[h * CHUNK : (h + 1) * CHUNK, :]
            ring(0, 1, e, True).start()
            ring(1, 1, e, True).start()
            for d in (2, 1, 3):
                row_copy(d, e, True).start()
        for e in range(PH):
            for way in range(2):
                ring(way, 1, e, False).wait_recv()
                ring(way, 2, e, True).start()

        @pl.when(it == 0)
        def _():
            loads[1].wait()

        for e in range(PH):
            for way in range(2):
                ring(way, 2, e, False).wait_recv()
                ring(way, 3, e, True).start()
        for e in range(PH):
            for d in (1, 3, 2):
                row_copy(d, e, False).wait_recv()
            half_part(e)
            for way in range(2):
                ring(way, 3, e, False).wait_recv()
                ring(way, 4, e, True).start()
        value = None
        for e in range(PH):
            for way in range(2):
                ring(way, 4, e, False).wait_recv()
            block = dot(half[e], panel[e])
            for h in range(2):
                cyc[2 * e + h] = (
                    block[:, h * TILE : (h + 1) * TILE]
                    .reshape(NX, ROWS, TILE)
                    .astype(BF16)
                )
            part = dot(
                perm_t[:, e * 256 : (e + 1) * 256],
                cyc[2 * e : 2 * e + 2].reshape(256, TILE),
            )
            value = part if value is None else value + part
        slotted[...] = value.reshape(NZ, NX, ZROWS, TILE).astype(BF16)
        for dz, dx in others:
            backward(dz, dx, True).start()
        back[z, x] = slotted[z, x]

        @pl.when(it == ITERS - 1)
        def _():
            for d in (2, 1, 3):
                own_copy(d, True).start()
            own_rows[x] = cyc[:, x]
            for d in (1, 3, 2):
                own_copy(d, False).wait_recv()
            for d in range(n_grp):
                owner = (g + d) % n_grp
                count = jnp.int32(0)
                first = jnp.int32(0)
                second = jnp.int32(0)
                for s in range(tile_list.shape[1]):
                    tile = tile_list[owner, s]
                    mine = tile // 24 == g
                    local = tile - g * 24
                    blk = local % 8
                    where = (blk % 4) * (2 * PH) + (local // 8) * 2 + blk // 4
                    first = jnp.where(mine & (count == 0), where, first)
                    second = jnp.where(mine & (count == 1), where, second)
                    count = count + jnp.where(mine, 1, 0)
                flat = own_rows.reshape(NX * 2 * PH, ROWS, TILE)
                if d == 0:
                    picked[g, 0] = flat[first]
                    picked[g, 1] = flat[second]
                else:
                    pick[d, 0] = flat[first]
                    pick[d, 1] = flat[second]
                    group_copy(d, True).start()

        for dz, dx in reversed(others):
            backward(dz, dx, False).wait_recv()
        together = jnp.concatenate(
            [back[:, xx].reshape(UNITS, TILE) for xx in range(NX)], axis=1
        )
        returned = dot(pack_t[...], together)
        for t in range(3):
            lanes = slice(t * SEG, (t + 1) * SEG)
            total = (amp[:, lanes].astype(F32) + ladder[:, lanes]) + returned[
                t * 64 : (t + 1) * 64, :
            ]
            doubles[t * 64 : (t + 1) * 64, :] = (
                total / (pair_e[:, lanes] + hole[:, :1])
            ).astype(BF16)

        for dz, dx in others:
            forward(dz, dx, True).wait_send()
            backward(dz, dx, True).wait_send()
        for e in range(PH):
            for d in range(1, NX):
                row_copy(d, e, True).wait_send()
            for step in range(1, 5):
                for way in range(2):
                    ring(way, step, e, True).wait_send()
        return carry

    lax.fori_loop(0, ITERS, iteration, jnp.int32(0))

    for t in range(3):
        d_out[:, t * SEG : (t + 1) * SEG] = doubles[t * 64 : (t + 1) * 64, :]

    for d in range(1, n_grp):
        group_copy(d, False).wait_recv()
    loads[2].wait()
    live = tile_count[g]
    flat = picked.reshape(n_grp * 2, ROWS, TILE)
    parts = []
    for s in range(tile_list.shape[1]):
        group = tile_list[g, s] // 24
        rank = jnp.int32(0)
        for before in range(s):
            rank = rank + jnp.where(tile_list[g, before] // 24 == group, 1, 0)
        part = flat[group * 2 + jnp.minimum(rank, 1)]
        parts.append(
            (part.astype(F32) * jnp.where(s < live, 1.0, 0.0).astype(F32)).astype(BF16)
        )
    t_out[...] = dot(jnp.concatenate(parts, axis=1), slab[...]).astype(BF16)

    for d in range(1, NX):
        slots_copy(d, True).wait_send()
        own_copy(d, True).wait_send()
    for d in range(1, n_grp):
        group_copy(d, True).wait_send()


def body(
    amplitudes,
    ladder_int,
    pair_energy,
    hole_energy,
    pack_map,
    unpack_map,
    coupling_index,
    coupling_table,
    cycle_int,
    tile_list,
    tile_count,
    slabs,
):
    n_grp = lax.axis_size("grp")
    width_p = amplitudes.shape[2]
    width_r = cycle_int.shape[1]
    vmem = pl.BlockSpec(memory_space=pltpu.VMEM)
    smem = pl.BlockSpec(memory_space=pltpu.SMEM)
    anywhere = pl.BlockSpec(memory_space=pl.ANY)
    dma = pltpu.SemaphoreType.DMA
    doubles, triples = pl.pallas_call(
        functools.partial(kernel, n_grp),
        out_shape=(
            jax.ShapeDtypeStruct((64, width_p), BF16),
            jax.ShapeDtypeStruct((ROWS, width_r), BF16),
        ),
        in_specs=[vmem] * 6 + [smem] * 3 + [anywhere] * 3,
        out_specs=(vmem, vmem),
        scratch_shapes=[
            pltpu.VMEM((PH, width_r, width_r), BF16),
            pltpu.VMEM((width_p, width_p), BF16),
            pltpu.VMEM((width_r, width_r), BF16),
            pltpu.VMEM((PH, TILE, 2 * TILE), BF16),
            pltpu.VMEM((NX, 1, UNITS), jnp.int32),
            pltpu.VMEM((64, TILE), F32),
            pltpu.VMEM((PLANE, PLANE), BF16),
            pltpu.VMEM((PLANE, PLANE), BF16),
            pltpu.VMEM((UNITS, UNITS), BF16),
            pltpu.VMEM((UNITS, UNITS), BF16),
            pltpu.VMEM((UNITS, SEG), BF16),
            pltpu.VMEM((64, width_p), F32),
            pltpu.VMEM((NZ, NX, ZROWS, TILE), BF16),
            pltpu.VMEM((NZ, NX, ZROWS, TILE), BF16),
            pltpu.VMEM((PH, width_r, 2 * TILE), BF16),
            pltpu.VMEM((NX, PH, CHUNK, 2 * TILE), BF16),
            pltpu.VMEM((PH, CHUNK, width_r), BF16),
            pltpu.VMEM((2 * PH, NX, ROWS, TILE), BF16),
            pltpu.VMEM((NZ, NX, ZROWS, TILE), BF16),
            pltpu.VMEM((NZ, NX, ZROWS, TILE), BF16),
            pltpu.VMEM((NX, 2 * PH, ROWS, TILE), BF16),
            pltpu.VMEM((n_grp, 2, ROWS, TILE), BF16),
            pltpu.VMEM((n_grp, 2, ROWS, TILE), BF16),
            dma((3,)),
            dma((2, NX)),
            dma((2, NZ, NX)),
            dma((2, NX, PH)),
            dma((2, 2, 4, PH)),
            dma((2, NZ, NX)),
            dma((2, NX)),
            dma((2, n_grp)),
        ],
        compiler_params=pltpu.CompilerParams(
            collective_id=0, has_side_effects=True, vmem_limit_bytes=60 * 1024 * 1024
        ),
    )(
        amplitudes[0],
        pair_energy,
        hole_energy,
        pack_map.reshape(1, -1),
        unpack_map.reshape(1, -1),
        coupling_index,
        coupling_table,
        tile_list,
        tile_count,
        cycle_int,
        ladder_int[0],
        slabs.reshape(width_r, width_r),
    )
    return doubles[None], triples[None]


def solution(mesh):
    return jax.shard_map(
        body,
        mesh=mesh,
        in_specs=(
            P("grp", "col", None),
            P("grp", None, None),
            P("grp", None),
            P("grp", "col"),
            P("col"),
            P("col"),
            P("grp", None, None),
            P(),
            P("grp", None, None),
            P(),
            P(),
            P("grp", None, None, None),
        ),
        out_specs=(P("grp", "col", None), P("grp", "col", None)),
        check_vma=False,
    )
```

```python
import functools

import jax
import jax.numpy as jnp
from jax import lax
from jax.experimental import pallas as pl
from jax.experimental.pallas import tpu as pltpu
from jax.sharding import PartitionSpec as P

MULT = 16
SEG = 512
TILE = 128
ITERS = 4
NX = 4
NZ = 8
PER = 6
ZROWS = NX * PER
UNITS = 192
PLANE = NX * UNITS
ROWS = 32
CHUNK = NX * ROWS
PH = 3
MESH = pl.DeviceIdType.MESH
F32 = jnp.float32
BF16 = jnp.bfloat16


def dot(a, b):
    return jnp.dot(a, b, preferred_element_type=F32)


def kernel(
    n_grp,
    amp,
    pair_e,
    hole_e,
    pack_row,
    unpack_row,
    coef_index,
    table,
    tile_list,
    tile_count,
    w_hbm,
    l_hbm,
    slab_hbm,
    d_out,
    t_out,
    w,
    lint,
    slab,
    kron,
    slots,
    perm,
    perm_t,
    pack,
    pack_t,
    doubles,
    ladder,
    amp_out,
    amp_in,
    mark_out,
    mark_in,
    ladder_out,
    ladder_in,
    slotted,
    back,
    current,
    start,
    source,
    denom,
    panel,
    rows_in,
    half,
    cyc,
    own_rows,
    pick,
    picked,
    local_sem,
    slots_sem,
    amp_sem,
    mark_sem,
    ladder_sem,
    back_sem,
    row_sem,
    ring_sem,
    tx_sem,
    tg_sem,
):
    me = lax.axis_index("col")
    g = lax.axis_index("grp")
    z = me // NX
    x = me % NX

    def at_z(d):
        return (z + d + NZ) % NZ

    def at_x(d):
        return (x + d + NX) % NX

    def remote(src, dst, sems, index, grp, zz, xx):
        return pltpu.make_async_remote_copy(
            src_ref=src,
            dst_ref=dst,
            send_sem=sems.at[(0,) + index],
            recv_sem=sems.at[(1,) + index],
            device_id=(grp, zz * NX + xx),
            device_id_type=MESH,
        )

    others = [(dz, dx) for dz in (4, 3, 5, 2, 6, 1, 7, 0) for dx in (2, 1, 3, 0)][:-1]

    loads = [
        pltpu.make_async_copy(l_hbm, lint, local_sem.at[0]),
        pltpu.make_async_copy(w_hbm, w, local_sem.at[1]),
        pltpu.make_async_copy(slab_hbm, slab, local_sem.at[2]),
    ]
    for load in loads:
        load.start()

    barrier = pltpu.get_barrier_semaphore()
    for dz, dx in others:
        pl.semaphore_signal(
            barrier, inc=1, device_id=(g, at_z(dz) * NX + at_x(dx)), device_id_type=MESH
        )
    for d in range(1, n_grp):
        pl.semaphore_signal(
            barrier, inc=1, device_id=((g + d) % n_grp, me), device_id_type=MESH
        )

    def iota(shape, axis):
        return lax.broadcasted_iota(jnp.int32, shape, axis)

    def one_hot(match):
        return match.astype(F32).astype(BF16)

    def as_column(row):
        size = row.shape[1]
        eye = iota((size, size), 0) == iota((size, size), 1)
        return jnp.sum(jnp.where(eye, row, 0.0), axis=1, keepdims=True)

    pack_line = pack_row[...].astype(F32)
    lane_k = iota((UNITS, UNITS), 1)
    row_k = iota((UNITS, UNITS), 0)
    lane_k = (lane_k % 64) * 3 + lane_k // 64
    row_k = (row_k % 64) * 3 + row_k // 64
    pack[...] = one_hot(as_column(pack_line) == lane_k.astype(F32))
    for t in range(3):
        doubles[t * 64 : (t + 1) * 64, :] = amp[:, t * SEG : (t + 1) * SEG]

    pl.semaphore_wait(barrier, len(others) + (n_grp - 1))

    def slots_copy(d, to):
        return remote(
            unpack_row, slots.at[x if to else at_x(-d)], slots_sem, (d,), g, z, at_x(d)
        )

    def exchange(src, dst, sems, dz, dx, to):
        zz, xx = at_z(dz), at_x(dx)
        place = dst.at[z, x] if to else dst.at[at_z(-dz), at_x(-dx)]
        return remote(src.at[zz, xx], place, sems, (dz, dx), g, zz, xx)

    def start_all(src, dst, sems):
        for dz, dx in others:
            exchange(src, dst, sems, dz, dx, True).start()
        dst[z, x] = src[z, x]

    def receive_all(src, dst, sems):
        for dz, dx in reversed(others):
            exchange(src, dst, sems, dz, dx, False).wait_recv()

    def sent_all(src, dst, sems):
        for dz, dx in others:
            exchange(src, dst, sems, dz, dx, True).wait_send()

    def pack_into(dst, value):
        for zz in range(NZ):
            for xx in range(NX):
                dst[zz, xx] = value[
                    zz * ZROWS : (zz + 1) * ZROWS, xx * TILE : (xx + 1) * TILE
                ].astype(BF16)

    def ladder_part(t):
        acc = None
        for k in range(3):
            part = dot(
                doubles[k * 64 : (k + 1) * 64, :],
                lint[k * SEG : (k + 1) * SEG, t * SEG : (t + 1) * SEG],
            )
            acc = part if acc is None else acc + part
        ladder[t * 64 : (t + 1) * 64, :] = acc.astype(BF16)

    def send_ladder():
        pack_into(ladder_out, dot(pack[...], ladder[...]))
        start_all(ladder_out, ladder_in, ladder_sem)

    def row_copy(par, d, e, to):
        rows = pl.ds(pl.multiple_of(z * CHUNK, CHUNK), CHUNK)
        return remote(
            panel.at[par, e, rows, :],
            rows_in.at[par, x if to else at_x(-d), e],
            row_sem,
            (par, d, e),
            g,
            z,
            at_x(d),
        )

    def ring(par, way, step, e, to):
        sign = 1 if way == 0 else -1
        chunk = at_z(-sign * (step - 1)) if to else at_z(-sign * step)
        if step < 4:
            rows = pl.ds(pl.multiple_of(chunk * CHUNK, CHUNK), CHUNK)
        else:
            rows = pl.ds(pl.multiple_of(chunk * CHUNK + way * 64, 64), 64)
        ref = panel.at[par, e, rows, :]
        return remote(
            ref, ref, ring_sem, (par, way, step - 1, e), g, at_z(sign), x
        )

    def pass_on(par, step, e):
        for way in range(2):
            ring(par, way, step, e, False).wait_recv()
            ring(par, way, step + 1, e, True).start()

    def recouple(value, e):
        mixed = dot(value.astype(BF16), kron[e])
        return (value + (mixed[:, :TILE] + mixed[:, TILE:])).astype(BF16)

    def launch(par, e):
        done = recouple(current[e * 256 : (e + 1) * 256, :].astype(F32), e)
        rows = pl.ds(pl.multiple_of(z * CHUNK, CHUNK), CHUNK)
        for h in range(2):
            lanes = slice(h * TILE, (h + 1) * TILE)
            panel[par, e, rows, lanes] = done[h * CHUNK : (h + 1) * CHUNK, :]
            rows_in[par, x, e, :, lanes] = done[h * CHUNK : (h + 1) * CHUNK, :]
        ring(par, 0, 1, e, True).start()
        ring(par, 1, 1, e, True).start()
        for d in (2, 1, 3):
            row_copy(par, d, e, True).start()

    def half_part(par, e):
        value = jnp.concatenate(
            [
                rows_in[par, xx, e, :, h * TILE : (h + 1) * TILE]
                for h in range(2)
                for xx in range(NX)
            ],
            axis=1,
        )
        half[e] = dot(value, w[e]).astype(BF16)

    def unpacked():
        together = jnp.concatenate(
            [back[:, xx].reshape(UNITS, TILE) for xx in range(NX)], axis=1
        )
        return dot(pack_t[...], together).astype(BF16)

    def own_copy(d, to):
        target = at_x(d)
        return remote(
            cyc.at[:, target],
            own_rows.at[x if to else at_x(-d)],
            tx_sem,
            (d,),
            g,
            z,
            target,
        )

    def group_copy(d, to):
        target = (g + d) % n_grp
        source = g if to else (g - d + n_grp) % n_grp
        return remote(pick.at[d], picked.at[source], tg_sem, (d,), target, z, x)

    for d in range(1, NX):
        slots_copy(d, True).start()
    pack_into(amp_out, dot(pack[...], doubles[...]))
    start_all(amp_out, amp_in, amp_sem)
    slots[x] = unpack_row[...]

    pack_t[...] = one_hot(pack_line == row_k.astype(F32))

    def coef_step(k, acc):
        return jnp.where(coef_index[...] == k, table[k], acc)

    coefs = lax.fori_loop(
        0, table.shape[0], coef_step, jnp.zeros((PH, MULT, MULT), F32)
    )
    spread = one_hot(iota((TILE, MULT), 0) % MULT == iota((TILE, MULT), 1))
    same = iota((TILE, TILE), 0) // MULT == iota((TILE, TILE), 1) // MULT
    turned = (((1,), (1,)), ((), ()))
    for e in range(PH):
        high = coefs[e].astype(BF16)
        low = (coefs[e] - high.astype(F32)).astype(BF16)
        for i, part in enumerate((high, low)):
            tall = lax.dot_general(spread, part, turned, preferred_element_type=F32)
            full = lax.dot_general(
                tall.astype(BF16), spread, turned, preferred_element_type=F32
            )
            kron[e, :, i * TILE : (i + 1) * TILE] = jnp.where(same, full, 0.0).astype(
                BF16
            )

    for d in range(1, NX):
        slots_copy(d, False).wait_recv()
    raw = jnp.concatenate(
        [slots[xx] for xx in range(NX)] + [slots[xx] for xx in range(NX)], axis=0
    )
    raw = raw.astype(F32).astype(BF16)
    mine = iota((8, TILE), 0) == iota((8, TILE), 1) // ROWS
    owner = iota((1, TILE), 1) // ROWS
    for k in range(2 * PH):
        select = one_hot(
            iota((UNITS, TILE), 0) == (iota((UNITS, TILE), 1) % ROWS) * 2 * PH + k
        )
        found = jnp.where(mine, dot(raw, select), 0.0)
        unit = jnp.sum(found, axis=0, keepdims=True).astype(jnp.int32)
        line = (unit // PER) * ZROWS + unit % PER + owner * PER
        perm_t[:, k * TILE : (k + 1) * TILE] = one_hot(iota((PLANE, TILE), 0) == line)
        column = as_column(line.astype(F32)).astype(jnp.int32)
        perm[k * TILE : (k + 1) * TILE, :] = one_hot(iota((TILE, PLANE), 1) == column)

    receive_all(amp_out, amp_in, amp_sem)
    found = dot(perm[...], amp_in[...].reshape(PLANE, TILE)).astype(BF16)
    current[...] = found
    start[...] = found
    for e in range(PH):
        launch(0, e)

    loads[0].wait()
    for t in range(3):
        ladder_part(t)
    send_ladder()

    hole = as_column(hole_e[...])
    hole_a = hole.astype(BF16).astype(F32)
    hole_b = (hole - hole_a).astype(BF16).astype(F32)
    hole_c = hole - hole_a - hole_b
    lane = iota((64, TILE), 1)
    marks = []
    for t in range(3):
        mark = jnp.where(lane == 3 + t, 1.0, 0.0)
        mark = jnp.where(lane == 0, hole_a, mark)
        mark = jnp.where(lane == 1, hole_b, mark)
        mark = jnp.where(lane == 2, hole_c, mark)
        marks.append(mark.astype(BF16))
    marked = dot(pack[...], jnp.concatenate(marks, axis=0))
    for zz in range(NZ):
        line = marked[zz * ZROWS : (zz + 1) * ZROWS, :].astype(BF16)
        for xx in range(NX):
            mark_out[zz, xx] = line
    start_all(mark_out, mark_in, mark_sem)
    for e in range(PH):
        pass_on(0, 1, e)
    loads[1].wait()
    receive_all(mark_out, mark_in, mark_sem)
    marked = dot(perm[...], mark_in[...].reshape(PLANE, TILE))
    pairs = jnp.zeros((PLANE, TILE), F32)
    for t in range(3):
        lanes = pl.ds(pl.multiple_of(t * SEG + x * TILE, TILE), TILE)
        pairs = pairs + marked[:, 3 + t : 4 + t] * pair_e[:, lanes]
    denom[...] = pairs + (marked[:, 0:1] + marked[:, 1:2] + marked[:, 2:3])

    def iteration(it, carry):
        par = it % 2

        @pl.when(it > 0)
        def _():
            for e in range(PH):
                pass_on(par, 1, e)

        for e in range(PH):
            for d in (1, 3, 2):
                row_copy(par, d, e, False).wait_recv()
            half_part(par, e)
            pass_on(par, 2, e)

        @pl.when(it > 0)
        def _():
            receive_all(slotted, back, back_sem)
            doubles[...] = unpacked()

        for e in range(PH):

            @pl.when(it > 0)
            def _():
                ladder_part(e)

            pass_on(par, 3, e)

        @pl.when(it > 0)
        def _():
            send_ladder()
            sent_all(slotted, back, back_sem)

        receive_all(ladder_out, ladder_in, ladder_sem)
        source[...] = dot(perm[...], ladder_in[...].reshape(PLANE, TILE)) + start[
            ...
        ].astype(F32)
        for e in range(PH):
            for way in range(2):
                ring(par, way, 4, e, False).wait_recv()
            block = dot(half[e], panel[par, e])
            for h in range(2):
                done = block[:, h * TILE : (h + 1) * TILE].astype(BF16)
                cyc[2 * e + h] = done.reshape(NX, ROWS, TILE)
                rows = slice((2 * e + h) * CHUNK, (2 * e + h + 1) * CHUNK)
                current[rows, :] = (
                    (source[rows, :] + done.astype(F32)) / denom[rows, :]
                ).astype(BF16)

            @pl.when(it < ITERS - 1)
            def _():
                launch((it + 1) % 2, e)

        @pl.when(it == ITERS - 1)
        def _():
            for d in (2, 1, 3):
                own_copy(d, True).start()

        slotted[...] = (
            dot(perm_t[...], current[...]).reshape(NZ, NX, ZROWS, TILE).astype(BF16)
        )
        start_all(slotted, back, back_sem)
        sent_all(ladder_out, ladder_in, ladder_sem)
        for e in range(PH):
            for d in range(1, NX):
                row_copy(par, d, e, True).wait_send()
            for step in range(1, 5):
                for way in range(2):
                    ring(par, way, step, e, True).wait_send()
        return carry

    lax.fori_loop(0, ITERS, iteration, jnp.int32(0))

    own_rows[x] = cyc[:, x]
    for d in (1, 3, 2):
        own_copy(d, False).wait_recv()
    for d in range(n_grp):
        owner = (g + d) % n_grp
        count = jnp.int32(0)
        first = jnp.int32(0)
        second = jnp.int32(0)
        for s in range(tile_list.shape[1]):
            tile = tile_list[owner, s]
            mine = tile // 24 == g
            local = tile - g * 24
            blk = local % 8
            where = (blk % 4) * (2 * PH) + (local // 8) * 2 + blk // 4
            first = jnp.where(mine & (count == 0), where, first)
            second = jnp.where(mine & (count == 1), where, second)
            count = count + jnp.where(mine, 1, 0)
        flat = own_rows.reshape(NX * 2 * PH, ROWS, TILE)
        if d == 0:
            picked[g, 0] = flat[first]
            picked[g, 1] = flat[second]
        else:
            pick[d, 0] = flat[first]
            pick[d, 1] = flat[second]
            group_copy(d, True).start()

    receive_all(slotted, back, back_sem)
    final = unpacked()
    for t in range(3):
        d_out[:, t * SEG : (t + 1) * SEG] = final[t * 64 : (t + 1) * 64, :]

    for d in range(1, n_grp):
        group_copy(d, False).wait_recv()
    loads[2].wait()
    live = tile_count[g]
    flat = picked.reshape(n_grp * 2, ROWS, TILE)
    parts = []
    for s in range(tile_list.shape[1]):
        group = tile_list[g, s] // 24
        rank = jnp.int32(0)
        for before in range(s):
            rank = rank + jnp.where(tile_list[g, before] // 24 == group, 1, 0)
        part = flat[group * 2 + jnp.minimum(rank, 1)]
        parts.append(
            (part.astype(F32) * jnp.where(s < live, 1.0, 0.0).astype(F32)).astype(BF16)
        )
    t_out[...] = dot(jnp.concatenate(parts, axis=1), slab[...]).astype(BF16)

    for d in range(1, NX):
        slots_copy(d, True).wait_send()
        own_copy(d, True).wait_send()
    for d in range(1, n_grp):
        group_copy(d, True).wait_send()
    sent_all(amp_out, amp_in, amp_sem)
    sent_all(mark_out, mark_in, mark_sem)
    sent_all(slotted, back, back_sem)


def body(
    amplitudes,
    ladder_int,
    pair_energy,
    hole_energy,
    pack_map,
    unpack_map,
    coupling_index,
    coupling_table,
    cycle_int,
    tile_list,
    tile_count,
    slabs,
):
    n_grp = lax.axis_size("grp")
    width_p = amplitudes.shape[2]
    width_r = cycle_int.shape[1]
    vmem = pl.BlockSpec(memory_space=pltpu.VMEM)
    smem = pl.BlockSpec(memory_space=pltpu.SMEM)
    anywhere = pl.BlockSpec(memory_space=pl.ANY)
    dma = pltpu.SemaphoreType.DMA
    doubles, triples = pl.pallas_call(
        functools.partial(kernel, n_grp),
        out_shape=(
            jax.ShapeDtypeStruct((64, width_p), BF16),
            jax.ShapeDtypeStruct((ROWS, width_r), BF16),
        ),
        in_specs=[vmem] * 6 + [smem] * 3 + [anywhere] * 3,
        out_specs=(vmem, vmem),
        scratch_shapes=[
            pltpu.VMEM((PH, width_r, width_r), BF16),
            pltpu.VMEM((width_p, width_p), BF16),
            pltpu.VMEM((width_r, width_r), BF16),
            pltpu.VMEM((PH, TILE, 2 * TILE), BF16),
            pltpu.VMEM((NX, 1, UNITS), jnp.int32),
            pltpu.VMEM((PLANE, PLANE), BF16),
            pltpu.VMEM((PLANE, PLANE), BF16),
            pltpu.VMEM((UNITS, UNITS), BF16),
            pltpu.VMEM((UNITS, UNITS), BF16),
            pltpu.VMEM((UNITS, SEG), BF16),
            pltpu.VMEM((UNITS, SEG), BF16),
        ]
        + [pltpu.VMEM((NZ, NX, ZROWS, TILE), BF16)] * 8
        + [
            pltpu.VMEM((PLANE, TILE), BF16),
            pltpu.VMEM((PLANE, TILE), BF16),
            pltpu.VMEM((PLANE, TILE), F32),
            pltpu.VMEM((PLANE, TILE), F32),
            pltpu.VMEM((2, PH, width_r, 2 * TILE), BF16),
            pltpu.VMEM((2, NX, PH, CHUNK, 2 * TILE), BF16),
            pltpu.VMEM((PH, CHUNK, width_r), BF16),
            pltpu.VMEM((2 * PH, NX, ROWS, TILE), BF16),
            pltpu.VMEM((NX, 2 * PH, ROWS, TILE), BF16),
            pltpu.VMEM((n_grp, 2, ROWS, TILE), BF16),
            pltpu.VMEM((n_grp, 2, ROWS, TILE), BF16),
            dma((3,)),
            dma((2, NX)),
            dma((2, NZ, NX)),
            dma((2, NZ, NX)),
            dma((2, NZ, NX)),
            dma((2, NZ, NX)),
            dma((2, 2, NX, PH)),
            dma((2, 2, 2, 4, PH)),
            dma((2, NX)),
            dma((2, n_grp)),
        ],
        compiler_params=pltpu.CompilerParams(
            collective_id=0, has_side_effects=True, vmem_limit_bytes=60 * 1024 * 1024
        ),
    )(
        amplitudes[0],
        pair_energy,
        hole_energy,
        pack_map.reshape(1, -1),
        unpack_map.reshape(1, -1),
        coupling_index,
        coupling_table,
        tile_list,
        tile_count,
        cycle_int,
        ladder_int[0],
        slabs.reshape(width_r, width_r),
    )
    return doubles[None], triples[None]


def solution(mesh):
    return jax.shard_map(
        body,
        mesh=mesh,
        in_specs=(
            P("grp", "col", None),
            P("grp", None, None),
            P("grp", None),
            P("grp", "col"),
            P("col"),
            P("col"),
            P("grp", None, None),
            P(),
            P("grp", None, None),
            P(),
            P(),
            P("grp", None, None, None),
        ),
        out_specs=(P("grp", "col", None), P("grp", "col", None)),
        check_vma=False,
    )
```

```python
import functools

import jax
import jax.numpy as jnp
from jax import lax
from jax.experimental import pallas as pl
from jax.experimental.pallas import tpu as pltpu
from jax.sharding import PartitionSpec as P

MULT = 16
SEG = 512
TILE = 128
ITERS = 4
NX = 4
NZ = 8
PER = 6
ZROWS = NX * PER
UNITS = 192
PLANE = NX * UNITS
ROWS = 32
CHUNK = NX * ROWS
PH = 3
MESH = pl.DeviceIdType.MESH
F32 = jnp.float32
BF16 = jnp.bfloat16


def dot(a, b):
    return jnp.dot(a, b, preferred_element_type=F32)


def kernel(
    n_grp,
    amp,
    pair_e,
    hole_e,
    pack_row,
    unpack_row,
    coef_index,
    table,
    tile_list,
    tile_count,
    w_hbm,
    l_hbm,
    slab_hbm,
    d_out,
    t_out,
    w,
    lint,
    slab,
    kron,
    slots,
    perm,
    perm_t,
    pack,
    pack_t,
    doubles,
    ladder,
    amp_out,
    amp_in,
    mark_out,
    mark_in,
    ladder_out,
    ladder_in,
    slotted,
    back,
    current,
    start,
    source,
    denom,
    panel,
    rows_in,
    half,
    cyc,
    own_rows,
    pick,
    picked,
    local_sem,
    slots_sem,
    amp_sem,
    mark_sem,
    ladder_sem,
    back_sem,
    row_sem,
    ring_sem,
    tx_sem,
    tg_sem,
):
    me = lax.axis_index("col")
    g = lax.axis_index("grp")
    z = me // NX
    x = me % NX

    def at_z(d):
        return (z + d + NZ) % NZ

    def at_x(d):
        return (x + d + NX) % NX

    def remote(src, dst, sems, index, grp, zz, xx):
        return pltpu.make_async_remote_copy(
            src_ref=src,
            dst_ref=dst,
            send_sem=sems.at[(0,) + index],
            recv_sem=sems.at[(1,) + index],
            device_id=(grp, zz * NX + xx),
            device_id_type=MESH,
        )

    others = [(dz, dx) for dz in (4, 3, 5, 2, 6, 1, 7, 0) for dx in (2, 1, 3, 0)][:-1]

    loads = [
        pltpu.make_async_copy(l_hbm, lint, local_sem.at[0]),
        pltpu.make_async_copy(w_hbm, w, local_sem.at[1]),
        pltpu.make_async_copy(slab_hbm, slab, local_sem.at[2]),
    ]
    for load in loads:
        load.start()

    barrier = pltpu.get_barrier_semaphore()
    for dz, dx in others:
        pl.semaphore_signal(
            barrier, inc=1, device_id=(g, at_z(dz) * NX + at_x(dx)), device_id_type=MESH
        )
    for d in range(1, n_grp):
        pl.semaphore_signal(
            barrier, inc=1, device_id=((g + d) % n_grp, me), device_id_type=MESH
        )

    def iota(shape, axis):
        return lax.broadcasted_iota(jnp.int32, shape, axis)

    def one_hot(match):
        return match.astype(F32).astype(BF16)

    def as_column(row):
        size = row.shape[1]
        eye = iota((size, size), 0) == iota((size, size), 1)
        return jnp.sum(jnp.where(eye, row, 0.0), axis=1, keepdims=True)

    pack_line = pack_row[...].astype(F32)
    lane_k = iota((UNITS, UNITS), 1)
    row_k = iota((UNITS, UNITS), 0)
    lane_k = (lane_k % 64) * 3 + lane_k // 64
    row_k = (row_k % 64) * 3 + row_k // 64
    pack[...] = one_hot(as_column(pack_line) == lane_k.astype(F32))
    for t in range(3):
        doubles[t * 64 : (t + 1) * 64, :] = amp[:, t * SEG : (t + 1) * SEG]

    pl.semaphore_wait(barrier, len(others) + (n_grp - 1))

    def slots_copy(d, to):
        return remote(
            unpack_row, slots.at[x if to else at_x(-d)], slots_sem, (d,), g, z, at_x(d)
        )

    def exchange(src, dst, sems, dz, dx, to):
        zz, xx = at_z(dz), at_x(dx)
        place = dst.at[z, x] if to else dst.at[at_z(-dz), at_x(-dx)]
        return remote(src.at[zz, xx], place, sems, (dz, dx), g, zz, xx)

    def start_all(src, dst, sems):
        for dz, dx in others:
            exchange(src, dst, sems, dz, dx, True).start()
        dst[z, x] = src[z, x]

    def receive_all(src, dst, sems):
        for dz, dx in reversed(others):
            exchange(src, dst, sems, dz, dx, False).wait_recv()

    def sent_all(src, dst, sems):
        for dz, dx in others:
            exchange(src, dst, sems, dz, dx, True).wait_send()

    def pack_into(dst, value):
        for zz in range(NZ):
            for xx in range(NX):
                dst[zz, xx] = value[
                    zz * ZROWS : (zz + 1) * ZROWS, xx * TILE : (xx + 1) * TILE
                ].astype(BF16)

    def ladder_part(t):
        acc = None
        for k in range(3):
            part = dot(
                doubles[k * 64 : (k + 1) * 64, :],
                lint[k * SEG : (k + 1) * SEG, t * SEG : (t + 1) * SEG],
            )
            acc = part if acc is None else acc + part
        ladder[t * 64 : (t + 1) * 64, :] = acc.astype(BF16)

    def send_ladder():
        pack_into(ladder_out, dot(pack[...], ladder[...]))
        start_all(ladder_out, ladder_in, ladder_sem)

    def row_copy(par, d, e, to):
        rows = pl.ds(pl.multiple_of(z * CHUNK, CHUNK), CHUNK)
        return remote(
            panel.at[par, e, rows, :],
            rows_in.at[par, x if to else at_x(-d), e],
            row_sem,
            (par, d, e),
            g,
            z,
            at_x(d),
        )

    def ring(par, way, step, e, to):
        sign = 1 if way == 0 else -1
        chunk = at_z(-sign * (step - 1)) if to else at_z(-sign * step)
        if step < 4:
            rows = pl.ds(pl.multiple_of(chunk * CHUNK, CHUNK), CHUNK)
        else:
            rows = pl.ds(pl.multiple_of(chunk * CHUNK + way * 64, 64), 64)
        ref = panel.at[par, e, rows, :]
        return remote(
            ref, ref, ring_sem, (par, way, step - 1, e), g, at_z(sign), x
        )

    def pass_on(par, step, e):
        for way in range(2):
            ring(par, way, step, e, False).wait_recv()
            ring(par, way, step + 1, e, True).start()

    def recouple(value, e):
        mixed = dot(value.astype(BF16), kron[e])
        return (value + (mixed[:, :TILE] + mixed[:, TILE:])).astype(BF16)

    def launch(par, e):
        done = recouple(current[e * 256 : (e + 1) * 256, :].astype(F32), e)
        rows = pl.ds(pl.multiple_of(z * CHUNK, CHUNK), CHUNK)
        for h in range(2):
            lanes = slice(h * TILE, (h + 1) * TILE)
            panel[par, e, rows, lanes] = done[h * CHUNK : (h + 1) * CHUNK, :]
            rows_in[par, x, e, :, lanes] = done[h * CHUNK : (h + 1) * CHUNK, :]
        ring(par, 0, 1, e, True).start()
        ring(par, 1, 1, e, True).start()
        for d in (2, 1, 3):
            row_copy(par, d, e, True).start()

    def half_part(par, e):
        value = jnp.concatenate(
            [
                rows_in[par, xx, e, :, h * TILE : (h + 1) * TILE]
                for h in range(2)
                for xx in range(NX)
            ],
            axis=1,
        )
        half[e] = dot(value, w[e]).astype(BF16)

    def unpacked():
        together = jnp.concatenate(
            [back[:, xx].reshape(UNITS, TILE) for xx in range(NX)], axis=1
        )
        return dot(pack_t[...], together).astype(BF16)

    def own_copy(d, to):
        target = at_x(d)
        return remote(
            cyc.at[:, target],
            own_rows.at[x if to else at_x(-d)],
            tx_sem,
            (d,),
            g,
            z,
            target,
        )

    def group_copy(d, to):
        target = (g + d) % n_grp
        source = g if to else (g - d + n_grp) % n_grp
        return remote(pick.at[d], picked.at[source], tg_sem, (d,), target, z, x)

    for d in range(1, NX):
        slots_copy(d, True).start()
    pack_into(amp_out, dot(pack[...], doubles[...]))
    start_all(amp_out, amp_in, amp_sem)
    slots[x] = unpack_row[...]

    loads[0].wait()
    for t in range(3):
        ladder_part(t)
    send_ladder()

    hole = as_column(hole_e[...])
    hole_a = hole.astype(BF16).astype(F32)
    hole_b = (hole - hole_a).astype(BF16).astype(F32)
    hole_c = hole - hole_a - hole_b
    lane = iota((64, TILE), 1)
    marks = []
    for t in range(3):
        mark = jnp.where(lane == 3 + t, 1.0, 0.0)
        mark = jnp.where(lane == 0, hole_a, mark)
        mark = jnp.where(lane == 1, hole_b, mark)
        mark = jnp.where(lane == 2, hole_c, mark)
        marks.append(mark.astype(BF16))
    marked = dot(pack[...], jnp.concatenate(marks, axis=0))
    for zz in range(NZ):
        line = marked[zz * ZROWS : (zz + 1) * ZROWS, :].astype(BF16)
        for xx in range(NX):
            mark_out[zz, xx] = line
    start_all(mark_out, mark_in, mark_sem)
    pack_t[...] = one_hot(pack_line == row_k.astype(F32))

    def coef_step(k, acc):
        return jnp.where(coef_index[...] == k, table[k], acc)

    coefs = lax.fori_loop(
        0, table.shape[0], coef_step, jnp.zeros((PH, MULT, MULT), F32)
    )
    spread = one_hot(iota((TILE, MULT), 0) % MULT == iota((TILE, MULT), 1))
    same = iota((TILE, TILE), 0) // MULT == iota((TILE, TILE), 1) // MULT
    turned = (((1,), (1,)), ((), ()))
    for e in range(PH):
        high = coefs[e].astype(BF16)
        low = (coefs[e] - high.astype(F32)).astype(BF16)
        for i, part in enumerate((high, low)):
            tall = lax.dot_general(spread, part, turned, preferred_element_type=F32)
            full = lax.dot_general(
                tall.astype(BF16), spread, turned, preferred_element_type=F32
            )
            kron[e, :, i * TILE : (i + 1) * TILE] = jnp.where(same, full, 0.0).astype(
                BF16
            )

    for d in range(1, NX):
        slots_copy(d, False).wait_recv()
    raw = jnp.concatenate(
        [slots[xx] for xx in range(NX)] + [slots[xx] for xx in range(NX)], axis=0
    )
    raw = raw.astype(F32).astype(BF16)
    mine = iota((8, TILE), 0) == iota((8, TILE), 1) // ROWS
    owner = iota((1, TILE), 1) // ROWS
    for k in range(2 * PH):
        select = one_hot(
            iota((UNITS, TILE), 0) == (iota((UNITS, TILE), 1) % ROWS) * 2 * PH + k
        )
        found = jnp.where(mine, dot(raw, select), 0.0)
        unit = jnp.sum(found, axis=0, keepdims=True).astype(jnp.int32)
        line = (unit // PER) * ZROWS + unit % PER + owner * PER
        perm_t[:, k * TILE : (k + 1) * TILE] = one_hot(iota((PLANE, TILE), 0) == line)
        column = as_column(line.astype(F32)).astype(jnp.int32)
        perm[k * TILE : (k + 1) * TILE, :] = one_hot(iota((TILE, PLANE), 1) == column)

    receive_all(amp_out, amp_in, amp_sem)
    found = dot(perm[...], amp_in[...].reshape(PLANE, TILE)).astype(BF16)
    current[...] = found
    start[...] = found
    for e in range(PH):
        launch(0, e)

    def iteration(it, carry):
        par = it % 2

        for e in range(PH):
            pass_on(par, 1, e)

        @pl.when(it == 0)
        def _():
            loads[1].wait()

        for e in range(PH):
            for d in (1, 3, 2):
                row_copy(par, d, e, False).wait_recv()
            half_part(par, e)

        @pl.when(it == 0)
        def _():
            receive_all(mark_out, mark_in, mark_sem)
            marked = dot(perm[...], mark_in[...].reshape(PLANE, TILE))
            pairs = jnp.zeros((PLANE, TILE), F32)
            for t in range(3):
                lanes = pl.ds(pl.multiple_of(t * SEG + x * TILE, TILE), TILE)
                pairs = pairs + marked[:, 3 + t : 4 + t] * pair_e[:, lanes]
            denom[...] = pairs + (marked[:, 0:1] + marked[:, 1:2] + marked[:, 2:3])

        @pl.when(it > 0)
        def _():
            receive_all(slotted, back, back_sem)
            doubles[...] = unpacked()
            ladder_part(0)

        pass_on(par, 2, 0)

        @pl.when(it > 0)
        def _():
            ladder_part(1)

        pass_on(par, 2, 1)

        @pl.when(it > 0)
        def _():
            ladder_part(2)
            send_ladder()

        pass_on(par, 2, 2)

        @pl.when(it > 0)
        def _():
            sent_all(slotted, back, back_sem)

        for e in range(PH):
            pass_on(par, 3, e)
        receive_all(ladder_out, ladder_in, ladder_sem)
        source[...] = dot(perm[...], ladder_in[...].reshape(PLANE, TILE)) + start[
            ...
        ].astype(F32)
        value = None
        for e in range(PH):
            for way in range(2):
                ring(par, way, 4, e, False).wait_recv()
            block = dot(half[e], panel[par, e])
            for h in range(2):
                done = block[:, h * TILE : (h + 1) * TILE].astype(BF16)
                cyc[2 * e + h] = done.reshape(NX, ROWS, TILE)
                rows = slice((2 * e + h) * CHUNK, (2 * e + h + 1) * CHUNK)
                current[rows, :] = (
                    (source[rows, :] + done.astype(F32)) / denom[rows, :]
                ).astype(BF16)

            part = dot(
                perm_t[:, e * 256 : (e + 1) * 256],
                current[e * 256 : (e + 1) * 256, :],
            )
            value = part if value is None else value + part
            if e == PH - 1:
                slotted[...] = value.reshape(NZ, NX, ZROWS, TILE).astype(BF16)
                start_all(slotted, back, back_sem)

            @pl.when(it < ITERS - 1)
            def _():
                launch((it + 1) % 2, e)

        @pl.when(it == ITERS - 1)
        def _():
            for d in (2, 1, 3):
                own_copy(d, True).start()

        sent_all(ladder_out, ladder_in, ladder_sem)
        for e in range(PH):
            for d in range(1, NX):
                row_copy(par, d, e, True).wait_send()
            for step in range(1, 5):
                for way in range(2):
                    ring(par, way, step, e, True).wait_send()
        return carry

    lax.fori_loop(0, ITERS, iteration, jnp.int32(0))

    own_rows[x] = cyc[:, x]
    for d in (1, 3, 2):
        own_copy(d, False).wait_recv()
    for d in range(n_grp):
        owner = (g + d) % n_grp
        count = jnp.int32(0)
        first = jnp.int32(0)
        second = jnp.int32(0)
        for s in range(tile_list.shape[1]):
            tile = tile_list[owner, s]
            mine = tile // 24 == g
            local = tile - g * 24
            blk = local % 8
            where = (blk % 4) * (2 * PH) + (local // 8) * 2 + blk // 4
            first = jnp.where(mine & (count == 0), where, first)
            second = jnp.where(mine & (count == 1), where, second)
            count = count + jnp.where(mine, 1, 0)
        flat = own_rows.reshape(NX * 2 * PH, ROWS, TILE)
        if d == 0:
            picked[g, 0] = flat[first]
            picked[g, 1] = flat[second]
        else:
            pick[d, 0] = flat[first]
            pick[d, 1] = flat[second]
            group_copy(d, True).start()

    receive_all(slotted, back, back_sem)
    final = unpacked()
    for t in range(3):
        d_out[:, t * SEG : (t + 1) * SEG] = final[t * 64 : (t + 1) * 64, :]

    for d in range(1, n_grp):
        group_copy(d, False).wait_recv()
    loads[2].wait()
    live = tile_count[g]
    flat = picked.reshape(n_grp * 2, ROWS, TILE)
    parts = []
    for s in range(tile_list.shape[1]):
        group = tile_list[g, s] // 24
        rank = jnp.int32(0)
        for before in range(s):
            rank = rank + jnp.where(tile_list[g, before] // 24 == group, 1, 0)
        part = flat[group * 2 + jnp.minimum(rank, 1)]
        parts.append(
            (part.astype(F32) * jnp.where(s < live, 1.0, 0.0).astype(F32)).astype(BF16)
        )
    t_out[...] = dot(jnp.concatenate(parts, axis=1), slab[...]).astype(BF16)

    for d in range(1, NX):
        slots_copy(d, True).wait_send()
        own_copy(d, True).wait_send()
    for d in range(1, n_grp):
        group_copy(d, True).wait_send()
    sent_all(amp_out, amp_in, amp_sem)
    sent_all(mark_out, mark_in, mark_sem)
    sent_all(slotted, back, back_sem)


def body(
    amplitudes,
    ladder_int,
    pair_energy,
    hole_energy,
    pack_map,
    unpack_map,
    coupling_index,
    coupling_table,
    cycle_int,
    tile_list,
    tile_count,
    slabs,
):
    n_grp = lax.axis_size("grp")
    width_p = amplitudes.shape[2]
    width_r = cycle_int.shape[1]
    vmem = pl.BlockSpec(memory_space=pltpu.VMEM)
    smem = pl.BlockSpec(memory_space=pltpu.SMEM)
    anywhere = pl.BlockSpec(memory_space=pl.ANY)
    dma = pltpu.SemaphoreType.DMA
    doubles, triples = pl.pallas_call(
        functools.partial(kernel, n_grp),
        out_shape=(
            jax.ShapeDtypeStruct((64, width_p), BF16),
            jax.ShapeDtypeStruct((ROWS, width_r), BF16),
        ),
        in_specs=[vmem] * 6 + [smem] * 3 + [anywhere] * 3,
        out_specs=(vmem, vmem),
        scratch_shapes=[
            pltpu.VMEM((PH, width_r, width_r), BF16),
            pltpu.VMEM((width_p, width_p), BF16),
            pltpu.VMEM((width_r, width_r), BF16),
            pltpu.VMEM((PH, TILE, 2 * TILE), BF16),
            pltpu.VMEM((NX, 1, UNITS), jnp.int32),
            pltpu.VMEM((PLANE, PLANE), BF16),
            pltpu.VMEM((PLANE, PLANE), BF16),
            pltpu.VMEM((UNITS, UNITS), BF16),
            pltpu.VMEM((UNITS, UNITS), BF16),
            pltpu.VMEM((UNITS, SEG), BF16),
            pltpu.VMEM((UNITS, SEG), BF16),
        ]
        + [pltpu.VMEM((NZ, NX, ZROWS, TILE), BF16)] * 8
        + [
            pltpu.VMEM((PLANE, TILE), BF16),
            pltpu.VMEM((PLANE, TILE), BF16),
            pltpu.VMEM((PLANE, TILE), F32),
            pltpu.VMEM((PLANE, TILE), F32),
            pltpu.VMEM((2, PH, width_r, 2 * TILE), BF16),
            pltpu.VMEM((2, NX, PH, CHUNK, 2 * TILE), BF16),
            pltpu.VMEM((PH, CHUNK, width_r), BF16),
            pltpu.VMEM((2 * PH, NX, ROWS, TILE), BF16),
            pltpu.VMEM((NX, 2 * PH, ROWS, TILE), BF16),
            pltpu.VMEM((n_grp, 2, ROWS, TILE), BF16),
            pltpu.VMEM((n_grp, 2, ROWS, TILE), BF16),
            dma((3,)),
            dma((2, NX)),
            dma((2, NZ, NX)),
            dma((2, NZ, NX)),
            dma((2, NZ, NX)),
            dma((2, NZ, NX)),
            dma((2, 2, NX, PH)),
            dma((2, 2, 2, 4, PH)),
            dma((2, NX)),
            dma((2, n_grp)),
        ],
        compiler_params=pltpu.CompilerParams(
            collective_id=0, has_side_effects=True, vmem_limit_bytes=60 * 1024 * 1024
        ),
    )(
        amplitudes[0],
        pair_energy,
        hole_energy,
        pack_map.reshape(1, -1),
        unpack_map.reshape(1, -1),
        coupling_index,
        coupling_table,
        tile_list,
        tile_count,
        cycle_int,
        ladder_int[0],
        slabs.reshape(width_r, width_r),
    )
    return doubles[None], triples[None]


def solution(mesh):
    return jax.shard_map(
        body,
        mesh=mesh,
        in_specs=(
            P("grp", "col", None),
            P("grp", None, None),
            P("grp", None),
            P("grp", "col"),
            P("col"),
            P("col"),
            P("grp", None, None),
            P(),
            P("grp", None, None),
            P(),
            P(),
            P("grp", None, None, None),
        ),
        out_specs=(P("grp", "col", None), P("grp", "col", None)),
        check_vma=False,
    )
```
